128 devices in a mesh: row: 8 (over y, core), col: 16 (over z, x).
Axes of the slice: x: 4, y: 4, z: 4, core: 2. Of those that a mesh axis runs over, the one named last changes fastest.
Arguments:
- wavefunction: bfloat16 [32, 16, 256, 256], P('row', 'col'), may hold values from -6 to 6
- env_left: bfloat16 [16, 32, 2, 256, 256], P('col', 'row'), may hold values from -0.25 to 0.25
- left_src: int32 [16, 32, 2], P('col', 'row'), may hold values from 0 to 3
- two_site: bfloat16 [16, 16, 16], P('col'), may hold values from -1.5 to 1.5
- env_right: bfloat16 [16, 32, 256, 256], P('col', 'row'), may hold values from -0.09375 to 0.09375
- right_loc: int32 [32, 16], P('row', 'col'), may hold values from 0 to 3
- left_size: int32 [32], P('row'), may hold values from 128 to 256
- right_size: int32 [32], P('row'), may hold values from 128 to 256
Outputs:
- applied: bfloat16 [32, 16, 256, 256], P('row', 'col')
The draws below stay inside these ranges and needn't reach their ends.
All inputs are finite; a program needn't handle non-finite values.
Results may differ from the reference program's by a relative error of at most 0.018.
Values may be sent and summed in bfloat16 or wider, within the bound.
No kernel may reach another device: no remote copies, remote signals or barrier semaphores. Data moves between devices by JAX's collectives and lax.ppermute only.
A program may use at most 128 MiB of HBM per device.

```python
import jax
import jax.numpy as jnp
from jax import lax

BT = 256
S = 16
LT_DEV = 4
RT_DEV = 4
K = 2
NL = 32
NR = 32
W = 16
TPG = 2


def touch_ends(result, own_key, low, high):
    spot = [jax.random.randint(jax.random.fold_in(own_key, axis), (), 0, length) for axis, length in enumerate(result.shape)]
    widest = result.shape.index(max(result.shape))
    neighbour = spot[:widest] + [(spot[widest] + 1) % result.shape[widest]] + spot[widest + 1:]
    return result.at[tuple(spot)].set(low).at[tuple(neighbour)].set(high)


def steps_of(rng, dims, split, least, top_value):
    factor_of, own = 1.0, jax.random.fold_in(rng, 6)
    for position, parts in split:
        steps = jnp.exp(jax.random.uniform(jax.random.fold_in(own, position), (parts,), jnp.float32, least / len(split), top_value / len(split)))
        factor_of = factor_of * jnp.repeat(steps, dims[position] // parts).reshape([-1 if axis == position else 1 for axis in range(len(dims))])
    return factor_of


def normal_values(stream_key, extent, deviation, most, cuts=(), held_as=jnp.bfloat16):
    entries = jax.random.normal(stream_key, extent, jnp.float32) * deviation
    if len(cuts) > 0:
        entries = steps_of(stream_key, extent, cuts, -0.22, 0.18) * entries
    return jnp.clip(entries, min=-most, max=most).astype(held_as)


def setup_inputs(seed: int = 0) -> dict:
    key_of = jax.random.split(jax.random.key(seed), 9)
    return {
        "wavefunction": normal_values(key_of[0], (NL, S, BT, BT), 1.0, 6.0, ((0, 8), (1, 16))),
        "env_left": normal_values(key_of[1], (W, NL, K, BT, BT), (K * BT) ** -0.5, 0.25, ((0, 16), (1, 8))),
        "left_src": touch_ends(jax.random.randint(key_of[2], (W, NL, K), 0, LT_DEV), jax.random.fold_in(key_of[2], 1), 0, LT_DEV - 1).astype(jnp.int32),
        "two_site": normal_values(key_of[3], (W, S, S), S ** -0.5, 1.5, ((0, 16),)),
        "env_right": normal_values(key_of[4], (W, NR, BT, BT), (BT * W) ** -0.5, 0.09375, ((0, 16), (1, 8))),
        "right_loc": touch_ends(jax.random.randint(key_of[5], (NL, S), 0, RT_DEV), jax.random.fold_in(key_of[5], 1), 0, RT_DEV - 1).astype(jnp.int32),
        "left_size": touch_ends(jax.random.randint(key_of[6], (NL,), BT // 2, BT + 1), jax.random.fold_in(key_of[6], 1), BT // 2, BT).astype(jnp.int32),
        "right_size": touch_ends(jax.random.randint(key_of[7], (NR,), BT // 2, BT + 1), jax.random.fold_in(key_of[7], 1), BT // 2, BT).astype(jnp.int32),
    }


def reference(wavefunction, env_left, left_src, two_site, env_right, right_loc, left_size, right_size):
    offsets = (jnp.arange(NL, dtype=jnp.int32) // LT_DEV) * LT_DEV
    sources = (offsets[None, :, None] + left_src).astype(jnp.int32)
    groups = (jnp.arange(S, dtype=jnp.int32) // TPG) * RT_DEV
    tile_ids = (groups[None, :] + right_loc).astype(jnp.int32)
    col_limit = right_size[tile_ids]
    col_iota = lax.broadcasted_iota(jnp.int32, (NL, S, BT, BT), 3)
    inside_cols = col_iota < col_limit[:, :, None, None]

    def one_term(total, inputs):
        left_w, source_w, site_w, right_w = inputs
        blocks = wavefunction[source_w]
        left_part = jnp.einsum("akxy,aksyz->asxz", left_w.astype(jnp.float32), blocks.astype(jnp.float32)).astype(jnp.bfloat16)
        left_part = lax.optimization_barrier(left_part)
        mixed = jnp.einsum("ts,asxz->atxz", site_w.astype(jnp.float32), left_part.astype(jnp.float32)).astype(jnp.bfloat16)
        mixed = lax.optimization_barrier(mixed)
        chosen = right_w[tile_ids]
        product = jnp.einsum("atxy,atzy->atxz", mixed.astype(jnp.float32), chosen.astype(jnp.float32))
        term = jnp.where(inside_cols, product, jnp.zeros_like(product)).astype(jnp.bfloat16)
        term = lax.optimization_barrier(term)
        return total + term.astype(jnp.float32), None

    start = jnp.zeros((NL, S, BT, BT), jnp.float32)
    total, _ = lax.scan(one_term, start, (env_left, sources, two_site, env_right))
    row_iota = lax.broadcasted_iota(jnp.int32, (NL, S, BT, BT), 2)
    inside_rows = row_iota < left_size[:, None, None, None]
    return jnp.where(inside_rows, total, jnp.zeros_like(total)).astype(jnp.bfloat16)
```

```python
import functools

import jax
import jax.numpy as jnp
from jax import lax
from jax.experimental import pallas as pl
from jax.experimental.pallas import tpu as pltpu
from jax.sharding import PartitionSpec as P

BAND = 16


def apply_kernel(src_ref, loc_ref, x_ref, left_ref, mix_ref, right_ref, out_ref, part, mixed):
    a = pl.program_id(0)
    states, _, tile, _ = x_ref.shape
    per_group = states // right_ref.shape[0]
    for s in range(states):
        total = jnp.dot(
            left_ref[0, 0], x_ref[s, src_ref[a, 0]], preferred_element_type=jnp.float32
        )
        total += jnp.dot(
            left_ref[0, 1], x_ref[s, src_ref[a, 1]], preferred_element_type=jnp.float32
        )
        part[s] = total.astype(jnp.bfloat16)
    for band in range(tile // BAND):
        rows = pl.ds(band * BAND, BAND)
        stacked = part[:, rows, :].reshape(states * BAND, tile)
        product = jnp.dot(mix_ref[...], stacked, preferred_element_type=jnp.float32)
        mixed[:, rows, :] = product.astype(jnp.bfloat16).reshape(states, BAND, tile)
    for t in range(states):
        product = lax.dot_general(
            mixed[t],
            right_ref[t // per_group, loc_ref[a, t]],
            (((1,), (1,)), ((), ())),
            preferred_element_type=jnp.float32,
        )
        out_ref[t, 0] = product.astype(jnp.bfloat16)


def apply_terms(src, loc, x, left, mix, right):
    states, tiles, tile, _ = x.shape
    whole = lambda shape: pl.BlockSpec(
        shape, lambda a, *_: (0,) * len(shape), pipeline_mode=pl.Buffered(1)
    )
    return pl.pallas_call(
        apply_kernel,
        out_shape=jax.ShapeDtypeStruct((states, tiles, tile, tile), jnp.bfloat16),
        grid_spec=pltpu.PrefetchScalarGridSpec(
            num_scalar_prefetch=2,
            grid=(tiles,),
            in_specs=[
                whole(x.shape),
                pl.BlockSpec((1,) + left.shape[1:], lambda a, *_: (a, 0, 0, 0)),
                whole(mix.shape),
                whole(right.shape),
            ],
            out_specs=pl.BlockSpec((states, 1, tile, tile), lambda a, *_: (0, a, 0, 0)),
            scratch_shapes=[
                pltpu.VMEM((states, tile, tile), jnp.bfloat16),
                pltpu.VMEM((states, tile, tile), jnp.bfloat16),
            ],
        ),
        compiler_params=pltpu.CompilerParams(vmem_limit_bytes=50 << 20),
        name="apply_terms",
    )(src, loc, x, left, mix, right)


def per_device(
    wavefunction, env_left, left_src, two_site, env_right, right_loc, left_size, right_size
):
    tile = wavefunction.shape[3]
    whole = lax.all_gather(wavefunction[:, 0], "col", axis=0, tiled=False)
    row = lax.broadcasted_iota(jnp.int32, (1, tile, 1), 1)
    right = jnp.where(row < right_size[:, None, None], env_right[0], 0).astype(jnp.bfloat16)
    right = lax.all_gather(right, "row", axis=0, tiled=False)
    loc = lax.all_gather(right_loc, "col", axis=1, tiled=True)
    mix = jnp.kron(two_site[0], jnp.eye(BAND, dtype=jnp.bfloat16))
    terms = apply_terms(left_src[0], loc, whole, env_left[0], mix, right)
    summed = lax.psum_scatter(terms, "col", scatter_dimension=0, tiled=False)
    inside = row < left_size[:, None, None]
    return jnp.where(inside, summed, 0).astype(jnp.bfloat16)[:, None]


def solution(mesh):
    placed = (
        P("row", "col", None, None),
        P("col", "row", None, None, None),
        P("col", "row", None),
        P("col", None, None),
        P("col", "row", None, None),
        P("row", "col"),
        P("row"),
        P("row"),
    )
    return jax.shard_map(
        per_device,
        mesh=mesh,
        in_specs=placed,
        out_specs=P("row", "col", None, None),
        check_vma=False,
    )
```

```python
import jax
import jax.numpy as jnp
from jax import lax
from jax.experimental import pallas as pl
from jax.experimental.pallas import tpu as pltpu
from jax.sharding import PartitionSpec as P

BAND = 16
RING = 4
OFFSETS = (0, -1, 1, 2)


def shift(value, dz, dx):
    pairs = []
    for device in range(RING * RING):
        z, x = device // RING, device % RING
        pairs.append((device, (z + dz) % RING * RING + (x + dx) % RING))
    return lax.ppermute(value, "col", pairs)


def along(axis, step):
    return (step, 0) if axis == "z" else (0, step)


def ring_gather(block, axis):
    half = block.shape[0] // 2
    low = shift(block, *along(axis, 1))
    high = shift(block, *along(axis, -1))
    far_low = shift(low[:half], *along(axis, 1))
    far_high = shift(high[half:], *along(axis, -1))
    return block, low, high, far_low, far_high


def add(*parts):
    total = parts[0].astype(jnp.float32)
    for part in parts[1:]:
        total += part.astype(jnp.float32)
    return total.astype(jnp.bfloat16)


def ring_reduce(own, low, high, far_low, far_high, axis):
    half = far_low.shape[0]
    up = shift(far_low, *along(axis, 1))
    down = shift(far_high, *along(axis, -1))
    high = jnp.concatenate([add(high[:half], up), high[half:]])
    low = jnp.concatenate([low[:half], add(low[half:], down)])
    return add(own, shift(high, *along(axis, 1)), shift(low, *along(axis, -1)))


def apply_kernel(src_ref, pick_ref, *refs):
    pieces, (left_ref, mix_ref, right_ref), refs = refs[:10], refs[10:13], refs[13:]
    outs, (x_ref, part, mixed, sem) = refs[:10], refs[10:]
    tile = left_ref.shape[-1]
    states = RING * RING

    copies = []
    for number in range(10):
        first, piece = number < 5, number % 5
        tiles = pl.ds(0 if first else 2, 2)
        inner = pl.ds(0 if piece < 4 else 2, 2 if piece >= 3 else 4)
        outer = min(piece, 3)
        place = (outer, inner) if first else (inner, outer)
        copies.append(
            pltpu.make_async_copy(pieces[number], x_ref.at[place + (tiles,)], sem.at[number])
        )
    for copy in copies:
        copy.start()
    for copy in copies:
        copy.wait()

    def product_for(a):
        for s in range(states):
            i, k = s // RING, s % RING
            total = jnp.dot(
                left_ref[a, 0], x_ref[i, k, src_ref[a, 0]], preferred_element_type=jnp.float32
            )
            total += jnp.dot(
                left_ref[a, 1], x_ref[i, k, src_ref[a, 1]], preferred_element_type=jnp.float32
            )
            part[s] = total.astype(jnp.bfloat16)
        for band in range(tile // BAND):
            rows = pl.ds(band * BAND, BAND)
            stacked = part[:, rows, :].reshape(states * BAND, tile)
            product = jnp.dot(mix_ref[...], stacked, preferred_element_type=jnp.float32)
            mixed[:, rows, :] = product.astype(jnp.bfloat16).reshape(states, BAND, tile)

    def store_for(a, first):
        outs_half = outs[:5] if first else outs[5:]
        for t in range(states):
            i, k = t // RING, t % RING
            outer, inner = (i, k) if first else (k, i)
            product = lax.dot_general(
                mixed[t],
                right_ref[pick_ref[a, t]],
                (((1,), (1,)), ((), ())),
                preferred_element_type=jnp.float32,
            ).astype(jnp.bfloat16)
            slot = a if first else a - 2
            if outer < 3:
                outs_half[outer][inner, slot] = product
            else:
                outs_half[3 + inner // 2][inner % 2, slot] = product

    for half in range(2):

        def body(step, carry):
            a = step + 2 * half
            product_for(a)
            store_for(a, half == 0)
            return carry

        lax.fori_loop(0, 2, body, 0)


def apply_terms(src, pick, pieces, left, mix, right):
    tile = left.shape[-1]
    out = lambda n: jax.ShapeDtypeStruct((n, 2, tile, tile), jnp.bfloat16)
    anywhere = pl.BlockSpec(memory_space=pl.ANY)
    vmem = pl.BlockSpec(memory_space=pltpu.VMEM)
    smem = pl.BlockSpec(memory_space=pltpu.SMEM)
    return pl.pallas_call(
        apply_kernel,
        out_shape=[out(RING)] * 3 + [out(2)] * 2 + [out(RING)] * 3 + [out(2)] * 2,
        in_specs=[smem, smem] + [anywhere] * 10 + [vmem] * 3,
        out_specs=[vmem] * 10,
        scratch_shapes=[
            pltpu.VMEM((RING, RING, 4, tile, tile), jnp.bfloat16),
            pltpu.VMEM((RING * RING, tile, tile), jnp.bfloat16),
            pltpu.VMEM((RING * RING, tile, tile), jnp.bfloat16),
            pltpu.SemaphoreType.DMA((10,)),
        ],
        compiler_params=pltpu.CompilerParams(vmem_limit_bytes=50 << 20),
        name="apply_terms",
    )(src, pick, *pieces, left, mix, right)


def per_device(
    wavefunction, env_left, left_src, two_site, env_right, right_loc, left_size, right_size
):
    tile = wavefunction.shape[3]
    states = two_site.shape[1]
    tiles = wavefunction.shape[0]
    z, x = lax.axis_index("col") // RING, lax.axis_index("col") % RING
    offsets = jnp.asarray(OFFSETS, jnp.int32)
    order = (
        ((z + offsets) % RING)[:, None] * RING + ((x + offsets) % RING)[None, :]
    ).reshape(states)

    row = lax.broadcasted_iota(jnp.int32, (1, tile, 1), 1)
    right = jnp.where(row < right_size[:, None, None], env_right[0], 0).astype(jnp.bfloat16)
    right = lax.all_gather(right, "row", axis=0, tiled=True)

    shard = wavefunction[:, 0]
    first = ring_gather(shard[:2], "x")
    second = ring_gather(shard[2:], "z")
    first = ring_gather(jnp.concatenate(first), "z")
    second = ring_gather(jnp.concatenate(second), "x")
    pieces = [p.reshape(-1, 2, tile, tile) for p in first + second]

    loc = lax.all_to_all(
        jnp.broadcast_to(right_loc[:, 0][None], (states, tiles)), "col", 0, 0, tiled=True
    )
    pick = ((order // 2 * 4)[:, None] + loc[order]).T
    mix = two_site[0][order][:, order]
    mix = jnp.kron(mix, jnp.eye(BAND, dtype=jnp.bfloat16))

    outs = apply_terms(left_src[0], pick, pieces, env_left[0], mix, right)
    own, low, high, far_low, far_high = outs[:5]
    sum_first = ring_reduce(own, low, high, far_low, far_high, "z")
    own, low, high, far_low, far_high = outs[5:]
    sum_second = ring_reduce(own, low, high, far_low, far_high, "x")

    def last(sums, axis):
        split = lambda v: v.reshape(2 * 2, tile // 2, tile)
        far = split(sums[3])
        return ring_reduce(
            split(sums[0]), split(sums[1]), split(sums[2]), far[:2], far[2:], axis
        ).reshape(2, tile, tile)

    summed = jnp.concatenate([last(sum_first, "x"), last(sum_second, "z")])
    inside = row < left_size[:, None, None]
    return jnp.where(inside, summed, 0).astype(jnp.bfloat16)[:, None]


def solution(mesh):
    placed = (
        P("row", "col", None, None),
        P("col", "row", None, None, None),
        P("col", "row", None),
        P("col", None, None),
        P("col", "row", None, None),
        P("row", "col"),
        P("row"),
        P("row"),
    )
    return jax.shard_map(
        per_device,
        mesh=mesh,
        in_specs=placed,
        out_specs=P("row", "col", None, None),
        check_vma=False,
    )
```

```python
import functools

import jax
import jax.numpy as jnp
from jax import lax
from jax.experimental import pallas as pl
from jax.experimental.pallas import tpu as pltpu
from jax.sharding import PartitionSpec as P

BAND = 16
RING = 4
STATES = RING * RING
OFFSETS = (0, -1, 1, 2)
LIMIT = 40 << 20


def shift(value, axis, step):
    pairs = []
    for device in range(STATES):
        z, x = device // RING, device % RING
        if axis == "z":
            z = (z + step) % RING
        else:
            x = (x + step) % RING
        pairs.append((device, z * RING + x))
    return lax.ppermute(value, "col", pairs)


def gather_near(block, axis):
    low = shift(block, axis, 1)
    high = shift(block, axis, -1)
    far = shift(block, axis, 2)
    return jnp.stack([block, low]), jnp.stack([high, far])


def gather_ring(first, second, axis):
    low_first = shift(first, axis, 1)
    high_second = shift(second, axis, -1)
    high_first = shift(first, axis, -1)
    low_second = shift(second, axis, 1)
    far_first = shift(low_first, axis, 1)
    far_second = shift(high_second, axis, -1)
    return (low_first, low_second), (high_first, high_second), (far_first, far_second)


def add(*parts):
    total = parts[0].astype(jnp.float32)
    for part in parts[1:]:
        total += part.astype(jnp.float32)
    return total.astype(jnp.bfloat16)


def left_product(left_ref, src_ref, a, pair):
    total = None
    for k in range(2):
        j = src_ref[a, k]
        both = jnp.concatenate([pair[0, j], pair[1, j]], axis=1)
        product = jnp.dot(left_ref[k], both, preferred_element_type=jnp.float32)
        total = product if total is None else total + product
    return total.astype(jnp.bfloat16)


def left_kernel(count, src_ref, left_ref, *refs):
    pairs, outs = refs[:count], refs[count:]

    def body(a, carry):
        for pair, out in zip(pairs, outs):
            out[a] = left_product(left_ref.at[a], src_ref, a, pair)
        return carry

    lax.fori_loop(0, left_ref.shape[0], body, 0)


def left_parts(src, left, pairs):
    tiles, _, tile, _ = left.shape
    smem = pl.BlockSpec(memory_space=pltpu.SMEM)
    vmem = pl.BlockSpec(memory_space=pltpu.VMEM)
    count = len(pairs)
    return pl.pallas_call(
        functools.partial(left_kernel, count),
        out_shape=[jax.ShapeDtypeStruct((tiles, tile, tile), jnp.bfloat16)] * count,
        in_specs=[smem] + [vmem] * (count + 1),
        out_specs=[vmem] * count,
        compiler_params=pltpu.CompilerParams(vmem_limit_bytes=20 << 20),
        cost_estimate=pl.CostEstimate(
            flops=count * tiles * 2 * 2 * tile**3,
            bytes_accessed=count * tiles * tile * tile * 4,
            transcendentals=0,
        ),
        name="left_parts",
    )(src, left, *pairs)


def right_product(block, right, pick):
    return lax.dot_general(
        block, right[pick], (((1,), (1,)), ((), ())), preferred_element_type=jnp.float32
    ).astype(jnp.bfloat16)


def mix_kernel(src_ref, pick_ref, left_ref, mix_ref, right_hbm, *refs):
    far, near, refs = refs[:4], refs[4:16], refs[16:]
    mixed_ref, far_outs, (own, right, sem) = refs[0], refs[1:5], refs[5:]
    a = pl.program_id(0)
    tile = left_ref.shape[-1]
    fetch = pltpu.make_async_copy(right_hbm, right, sem)

    @pl.when(a == 0)
    def _():
        fetch.start()

    for number in range(4):
        own[number] = left_product(left_ref.at[0], src_ref, a, far[number])

    def slab(half, ring, inner, rows):
        lanes = pl.ds(inner % 2 * (tile // 2), tile // 2)
        if ring == 3:
            return own[half * 2 + inner // 2, rows, lanes]
        return near[(half * 3 + ring) * 2 + inner // 2][0, rows, lanes]

    for band in range(tile // BAND):
        rows = pl.ds(band * BAND, BAND)
        slabs = []
        for s in range(STATES):
            i, k = s // RING, s % RING
            slabs.append(jnp.concatenate([slab(0, i, k, rows), slab(1, k, i, rows)], axis=1))
        product = jnp.dot(
            mix_ref[...], jnp.concatenate(slabs), preferred_element_type=jnp.float32
        )
        mixed_ref[0, :, rows, :] = product.astype(jnp.bfloat16).reshape(STATES, BAND, tile)

    @pl.when(a == 0)
    def _():
        fetch.wait()

    for half in range(2):

        @pl.when(a // 2 == half)
        def _():
            for inner in range(RING):
                t = 3 * RING + inner if half == 0 else inner * RING + 3
                far_outs[half * 2 + inner // 2][inner % 2, 0] = right_product(
                    mixed_ref[0, t], right, pick_ref[a, t]
                )


def term_kernel(pick_ref, mixed_ref, right, *outs):
    a = pl.program_id(0)
    for half in range(2):

        @pl.when(a // 2 == half)
        def _():
            for ring in (2, 1, 0):
                for inner in range(RING):
                    t = ring * RING + inner if half == 0 else inner * RING + ring
                    product = right_product(mixed_ref[0, t], right, pick_ref[a, t])
                    if ring:
                        outs[half * 8 + (ring - 1) * 2 + inner // 2][inner % 2, 0] = product
                    else:
                        outs[half * 8 + 4 + inner][0] = product


def half_slot(half):
    return lambda a: jnp.minimum(a, 1) if half == 0 else jnp.maximum(a - 2, 0)


def whole(shape):
    return pl.BlockSpec(shape, lambda a: (0,) * len(shape), pipeline_mode=pl.Buffered(1))


def pair_spec(half, tile):
    slot = half_slot(half)
    return pl.BlockSpec((2, 1, tile, tile), lambda a: (0, slot(a), 0, 0))


def mixed_and_far(src, pick, left, mix, right, far, near):
    tiles, _, tile, _ = left.shape
    smem = pl.BlockSpec(memory_space=pltpu.SMEM)
    pair = jax.ShapeDtypeStruct((2, tiles // 2, tile, tile), jnp.bfloat16)
    return pl.pallas_call(
        mix_kernel,
        grid=(tiles,),
        out_shape=[jax.ShapeDtypeStruct((tiles, STATES, tile, tile), jnp.bfloat16)] + [pair] * 4,
        in_specs=[
            smem,
            smem,
            pl.BlockSpec((1, 2, tile, tile), lambda a: (a, 0, 0, 0)),
            whole(mix.shape),
            pl.BlockSpec(memory_space=pl.ANY),
        ]
        + [whole(far[0].shape)] * 4
        + [pl.BlockSpec((1, tile, tile), lambda a: (a, 0, 0))] * 12,
        out_specs=[pl.BlockSpec((1, STATES, tile, tile), lambda a: (a, 0, 0, 0))]
        + [pair_spec(half, tile) for half in (0, 0, 1, 1)],
        scratch_shapes=[
            pltpu.VMEM((4, tile, tile), jnp.bfloat16),
            pltpu.VMEM(right.shape, jnp.bfloat16),
            pltpu.SemaphoreType.DMA,
        ],
        compiler_params=pltpu.CompilerParams(vmem_limit_bytes=LIMIT),
        name="mixed_and_far",
    )(src, pick, left, mix, right, *far, *near)


def near_terms(pick, mixed, right):
    tiles, _, tile, _ = mixed.shape
    smem = pl.BlockSpec(memory_space=pltpu.SMEM)
    pair = jax.ShapeDtypeStruct((2, tiles // 2, tile, tile), jnp.bfloat16)
    single = jax.ShapeDtypeStruct((tiles // 2, tile, tile), jnp.bfloat16)

    def single_spec(half):
        slot = half_slot(half)
        return pl.BlockSpec((1, tile, tile), lambda a: (slot(a), 0, 0))

    return pl.pallas_call(
        term_kernel,
        grid=(tiles,),
        out_shape=([pair] * 4 + [single] * 4) * 2,
        in_specs=[
            smem,
            pl.BlockSpec((1, STATES, tile, tile), lambda a: (a, 0, 0, 0)),
            whole(right.shape),
        ],
        out_specs=[
            spec
            for half in (0, 1)
            for spec in [pair_spec(half, tile)] * 4 + [single_spec(half)] * 4
        ],
        compiler_params=pltpu.CompilerParams(vmem_limit_bytes=LIMIT),
        cost_estimate=pl.CostEstimate(
            flops=tiles * 12 * 2 * tile**3,
            bytes_accessed=tiles * 32 * 2 * tile * tile,
            transcendentals=0,
        ),
        name="near_terms",
    )(pick, mixed, right)


def ring_sums(far, near, axis):
    low_first, low_second, high_first, high_second = near[:4]
    own = near[4:]
    up = shift(far[0], axis, 1)
    down = shift(far[1], axis, -1)
    from_low_second = shift(high_second, axis, 1)
    from_high_first = shift(low_first, axis, -1)
    from_low_first = shift(add(high_first, up), axis, 1)
    from_high_second = shift(add(low_second, down), axis, -1)
    first = [add(own[n], from_high_first[n], from_low_first[n]) for n in range(2)]
    second = [add(own[2 + n], from_low_second[n], from_high_second[n]) for n in range(2)]
    return first + second


def last_sum(blocks, axis):
    own, low, high, far = blocks
    return (
        own,
        shift(far, axis, 2),
        shift(high, axis, 1),
        shift(low, axis, -1),
    )


def per_device(
    wavefunction, env_left, left_src, two_site, env_right, right_loc, left_size, right_size
):
    tile = wavefunction.shape[3]
    tiles = wavefunction.shape[0]
    z, x = lax.axis_index("col") // RING, lax.axis_index("col") % RING
    offsets = jnp.asarray(OFFSETS, jnp.int32)
    order = (
        ((z + offsets) % RING)[:, None] * RING + ((x + offsets) % RING)[None, :]
    ).reshape(STATES)

    shard = wavefunction[:, 0]
    own_a = gather_near(shard[:, :, : tile // 2], "x")
    own_b = gather_near(shard[:, :, tile // 2 :], "z")
    ring_a = gather_ring(*own_a, "z")
    ring_b = gather_ring(*own_b, "x")

    row = lax.broadcasted_iota(jnp.int32, (1, tile, 1), 1)
    right = jnp.where(row < right_size[:, None, None], env_right[0], 0).astype(jnp.bfloat16)
    right = lax.all_gather(right, "row", axis=0, tiled=True)
    loc = lax.all_to_all(
        jnp.broadcast_to(right_loc[:, 0][None], (STATES, tiles)), "col", 0, 0, tiled=True
    )
    pick = ((order // 2 * 4)[:, None] + loc[order]).T
    mix = two_site[0][order][:, order]
    mix = jnp.kron(mix, jnp.eye(BAND, dtype=jnp.bfloat16))

    src, left = left_src[0], env_left[0]
    parts_own = left_parts(src, left, own_a + own_b)
    parts_near = left_parts(src, left, ring_a[0] + ring_a[1] + ring_b[0] + ring_b[1])
    near = parts_own[:2] + parts_near[:4] + parts_own[2:] + parts_near[4:]
    mixed, *far = mixed_and_far(src, pick, left, mix, right, ring_a[2] + ring_b[2], near)
    outs = near_terms(pick, mixed, right)

    sums_a = ring_sums(far[:2], outs[:8], "z")
    sums_b = ring_sums(far[2:], outs[8:], "x")
    parts_a = last_sum(sums_a, "x")
    parts_b = last_sum(sums_b, "z")
    summed = jnp.concatenate([add(*parts_a), add(*parts_b)])
    inside = row < left_size[:, None, None]
    return jnp.where(inside, summed, 0).astype(jnp.bfloat16)[:, None]


def solution(mesh):
    placed = (
        P("row", "col", None, None),
        P("col", "row", None, None, None),
        P("col", "row", None),
        P("col", None, None),
        P("col", "row", None, None),
        P("row", "col"),
        P("row"),
        P("row"),
    )
    return jax.shard_map(
        per_device,
        mesh=mesh,
        in_specs=placed,
        out_specs=P("row", "col", None, None),
        check_vma=False,
    )
```

```python
import functools

import jax
import jax.numpy as jnp
from jax import lax
from jax.experimental import pallas as pl
from jax.experimental.pallas import tpu as pltpu
from jax.sharding import PartitionSpec as P

BAND = 16
RING = 4
STATES = RING * RING
CORES = 2
LIMIT = 48 << 20
CALLS = ((0, 2), (1, 3))
AXIS = ((0, 0), (0, 1), (0, 2), (0, 3), (1, 0), (2, 0), (3, 0))
NEAR = ((1, 1), (1, 3), (3, 1), (3, 3))
FAR = ((1, 2), (2, 1), (2, 2), (2, 3), (3, 2))

HBM = pl.BlockSpec(memory_space=pltpu.HBM)
SMEM = pl.BlockSpec(memory_space=pltpu.SMEM)
VMEM = pl.BlockSpec(memory_space=pltpu.VMEM)


def in_hbm(value):
    return pltpu.with_memory_space_constraint(value, pltpu.HBM)


def hop(value, axis, distance=1):
    pairs = []
    for row in range(RING * CORES):
        for col in range(STATES):
            step = distance if row % CORES == 0 else -distance
            y, z, x = row // CORES, col // RING, col % RING
            y, z, x = (
                (v + (step if name == axis else 0)) % RING
                for name, v in (("y", y), ("z", z), ("x", x))
            )
            target = (y * CORES + row % CORES) * STATES + z * RING + x
            pairs.append((row * STATES + col, target))
    return lax.ppermute(value, ("row", "col"), pairs)


def send(value, axis, step):
    pairs = []
    for device in range(STATES):
        z, x = device // RING, device % RING
        if axis == "z":
            z = (z + step) % RING
        else:
            x = (x + step) % RING
        pairs.append((device, z * RING + x))
    return lax.ppermute(value, "col", pairs)


def swap_cores(value):
    return lax.ppermute(value, "row", [(r, r ^ 1) for r in range(RING * CORES)])


def add(*parts):
    total = parts[0].astype(jnp.float32)
    for part in parts[1:]:
        total += part.astype(jnp.float32)
    return total.astype(jnp.bfloat16)


def left_product(left, src_ref, a, block):
    rows = jnp.concatenate([block(src_ref[a, k]) for k in range(2)], axis=0)
    wide = jnp.concatenate([left[a, 0], left[a, 1]], axis=1)
    return jnp.dot(wide, rows, preferred_element_type=jnp.float32).astype(jnp.bfloat16)


def joined(first, second):
    return lambda j: jnp.concatenate([first[j], second[j]], axis=1)


def axis_kernel(src_ref, left_hbm, *refs):
    count = len(AXIS)
    blocks_hbm, out_hbm, (left, blocks, out, sem) = refs[:count], refs[count], refs[count + 1 :]
    get_left = pltpu.make_async_copy(left_hbm, left, sem.at[0])
    gets = [
        pltpu.make_async_copy(blocks_hbm[n], blocks.at[n], sem.at[1 + n]) for n in range(count)
    ]
    puts = [
        pltpu.make_async_copy(out.at[n], out_hbm.at[n], sem.at[1 + count + n])
        for n in range(count)
    ]
    get_left.start()
    for get in gets:
        get.start()
    get_left.wait()
    for n in range(count):
        gets[n].wait()
        for a in range(left.shape[0]):
            out[n, a] = left_product(left, src_ref, a, lambda j: blocks[n, j])
        puts[n].start()
    for put in puts:
        put.wait()


def near_kernel(src_ref, left_hbm, *refs):
    pieces_hbm, out_hbm, (left, pieces, out, sem) = refs[:4], refs[4], refs[5:]
    get_left = pltpu.make_async_copy(left_hbm, left, sem.at[0])
    gets = [pltpu.make_async_copy(pieces_hbm[n], pieces.at[n], sem.at[1 + n]) for n in range(4)]
    puts = [pltpu.make_async_copy(out.at[n], out_hbm.at[n], sem.at[5 + n]) for n in range(4)]
    for get in [get_left] + gets:
        get.start()
    for get in [get_left] + gets:
        get.wait()
    for n, (i, k) in enumerate(NEAR):
        block = joined(pieces.at[i // 2, k - 1], pieces.at[2 + k // 2, i - 1])
        for a in range(left.shape[0]):
            out[n, a] = left_product(left, src_ref, a, block)
        puts[n].start()
    for put in puts:
        put.wait()


def left_parts(kernel, count, src, left, pieces):
    tiles, _, tile, _ = left.shape
    out = (count, tiles, tile, tile)
    return pl.pallas_call(
        kernel,
        out_shape=pltpu.HBM(out, jnp.bfloat16),
        in_specs=[SMEM] + [HBM] * (1 + len(pieces)),
        out_specs=HBM,
        scratch_shapes=[
            pltpu.VMEM(left.shape, jnp.bfloat16),
            pltpu.VMEM((len(pieces),) + pieces[0].shape, jnp.bfloat16),
            pltpu.VMEM(out, jnp.bfloat16),
            pltpu.SemaphoreType.DMA((1 + len(pieces) + count,)),
        ],
        compiler_params=pltpu.CompilerParams(vmem_limit_bytes=LIMIT),
        cost_estimate=pl.CostEstimate(
            flops=count * tiles * 4 * tile**3, bytes_accessed=5 << 20, transcendentals=0
        ),
        name="left_parts",
    )(src, left, *(in_hbm(piece) for piece in pieces))


def mix_matrix(two_site, z, x, flow):
    size = STATES * BAND
    slot = lax.broadcasted_iota(jnp.int32, (size, STATES), 0) // BAND
    lane = lax.broadcasted_iota(jnp.int32, (size, STATES), 1)
    target = ((z + slot // RING) & 3) * RING + ((x + slot % RING) & 3)
    source = jnp.zeros_like(slot)
    for n, (i, k) in enumerate(AXIS + NEAR + FAR):
        state = ((z - flow * i) & 3) * RING + ((x - flow * k) & 3)
        source = jnp.where(slot == n, state, source)
    spread = lambda state: jnp.where(state == lane, 1.0, 0.0).astype(jnp.bfloat16)
    half = jnp.dot(spread(target), two_site, preferred_element_type=jnp.float32)
    full = lax.dot_general(
        half.astype(jnp.bfloat16),
        spread(source),
        (((1,), (1,)), ((), ())),
        preferred_element_type=jnp.float32,
    )
    row = lax.broadcasted_iota(jnp.int32, (size, size), 0)
    col = lax.broadcasted_iota(jnp.int32, (size, size), 1)
    return jnp.where(row % BAND == col % BAND, full, 0.0).astype(jnp.bfloat16)


def term(mixed, right, loc_ref, a, state, spot):
    z, x, y, core, flow = spot
    i, k = state
    t = ((z + i) & 3) * RING + ((x + k) & 3)
    group = t // 2
    other = (group + core) & 1
    back = (flow * (1 - 2 * other) * (y - group // CORES)) & 3
    tile = (other * RING + back) * 4 + loc_ref[t, 0, a]
    return jnp.dot(mixed, right[tile], preferred_element_type=jnp.float32).astype(jnp.bfloat16)


def spot_of():
    c, r = lax.axis_index("col"), lax.axis_index("row")
    core = r % CORES
    return c // RING, c % RING, r // CORES, core, 1 - 2 * core


def slot_state(half, ahead, inner):
    return (ahead, inner) if half == 0 else (inner, ahead)


def apply_kernel(chosen, src_ref, loc_ref, two_site_ref, token_ref, left_hbm, *refs):
    right_hbm, pieces_hbm, near_hbm, refs = refs[:8], refs[8:14], refs[14:16], refs[16:]
    outs, (left, right, first, second, part, mix, mixed, sem) = refs[:-8], refs[-8:]
    tile = left.shape[-1]
    spot = spot_of()
    z, x, _, _, flow = spot
    outs, passed = outs[:-1], outs[-1]
    passed[...] = token_ref[...]

    gets = [pltpu.make_async_copy(left_hbm, left, sem.at[0])]
    for which, pieces in enumerate((first, second)):
        behind, ahead, far = pieces_hbm[3 * which : 3 * which + 3]
        gets += [
            pltpu.make_async_copy(behind.at[1], pieces.at[0, 1], sem.at[1 + 3 * which]),
            pltpu.make_async_copy(ahead.at[1], pieces.at[2, 1], sem.at[2 + 3 * which]),
            pltpu.make_async_copy(far, pieces.at[1], sem.at[3 + 3 * which]),
        ]
    get_right = [
        pltpu.make_async_copy(right_hbm[n], right.at[pl.ds(4 * n, 4)], sem.at[7 + n])
        for n in range(8)
    ]
    get_near = [
        [
            pltpu.make_async_copy(
                near_hbm[0].at[:, a], part.at[place, pl.ds(0, 7)], sem.at[15 + 2 * place]
            ),
            pltpu.make_async_copy(
                near_hbm[1].at[:, a], part.at[place, pl.ds(7, 4)], sem.at[16 + 2 * place]
            ),
        ]
        for place, a in enumerate(chosen)
    ]
    for get in gets + get_near[0] + get_right:
        get.start()
    for later in get_near[1:]:
        for get in later:
            get.start()
    mix[...] = mix_matrix(two_site_ref[0], z, x, flow)
    for get in gets:
        get.wait()

    order = AXIS + NEAR + FAR
    for number, a in enumerate(chosen):
        half = a // 2
        for n, (i, k) in enumerate(FAR):
            block = joined(first.at[i - 1, k - 1], second.at[k - 1, i - 1])
            part[number, len(AXIS) + len(NEAR) + n] = left_product(left, src_ref, a, block)
        for get in get_near[number]:
            get.wait()
        for band in range(tile // BAND):
            rows = pl.ds(band * BAND, BAND)
            stacked = part[number, :, rows, :].reshape(STATES * BAND, tile)
            product = jnp.dot(mix[...], stacked, preferred_element_type=jnp.float32)
            mixed[:, rows, :] = product.astype(jnp.bfloat16).reshape(STATES, BAND, tile)
        if number == 0:
            for get in get_right:
                get.wait()
        for ring in (2, 3, 1, 0):
            for inner in range(RING):
                i, k = slot_state(half, (flow * ring) & 3, (flow * inner) & 3)
                outs[number * RING + ring][inner] = term(
                    mixed[i * RING + k], right, loc_ref, a, (i, k), spot
                )


def apply_terms(chosen, src, loc, two_site, token, left, right, pieces, near):
    tiles, _, tile, _ = left.shape
    count = len(chosen)
    out = jax.ShapeDtypeStruct((RING, tile, tile), jnp.bfloat16)
    side = (RING - 1, RING - 1) + pieces[0].shape[1:]
    return pl.pallas_call(
        functools.partial(apply_kernel, chosen),
        out_shape=[out] * (RING * count) + [jax.ShapeDtypeStruct(token.shape, token.dtype)],
        in_specs=[SMEM, SMEM, VMEM, VMEM] + [HBM] * 17,
        out_specs=[VMEM] * (RING * count + 1),
        scratch_shapes=[
            pltpu.VMEM(left.shape, jnp.bfloat16),
            pltpu.VMEM((32, tile, tile), jnp.bfloat16),
            pltpu.VMEM(side, jnp.bfloat16),
            pltpu.VMEM(side, jnp.bfloat16),
            pltpu.VMEM((count, STATES, tile, tile), jnp.bfloat16),
            pltpu.VMEM((STATES * BAND, STATES * BAND), jnp.bfloat16),
            pltpu.VMEM((STATES, tile, tile), jnp.bfloat16),
            pltpu.SemaphoreType.DMA((15 + 2 * count,)),
        ],
        compiler_params=pltpu.CompilerParams(vmem_limit_bytes=LIMIT),
        cost_estimate=pl.CostEstimate(
            flops=count * 80 * tile**3, bytes_accessed=8 << 20, transcendentals=0
        ),
        name="apply_terms",
    )(src, loc, two_site, token, left, *(in_hbm(v) for v in (*right, *pieces, *near)))


def ring_sum(blocks, axis):
    own, behind, far, ahead = blocks
    straight = hop(ahead, axis, -1)
    return own, straight, hop(add(behind, hop(far, axis, 1)), axis, 1)


def last_sum(tiles, axis):
    blocks = [
        jnp.stack([add(*(part[n] for part in parts)) for parts in tiles]) for n in range(RING)
    ]
    return add(*ring_sum(blocks, axis))


def per_device(
    wavefunction, env_left, left_src, two_site, env_right, right_loc, left_size, right_size
):
    tile = wavefunction.shape[3]
    tiles = wavefunction.shape[0]
    src, left = left_src[0], env_left[0]

    shard, cut = wavefunction[:, 0], tile // 2
    behind_x, behind_z = hop(shard, "x", 1), hop(shard, "z", 1)
    ahead_x, ahead_z = hop(shard, "x", -1), hop(shard, "z", -1)
    far_x, far_z = hop(behind_x, "x", 1), hop(behind_z, "z", 1)

    env_right, right_loc, _ = lax.optimization_barrier((env_right, right_loc, behind_x))
    lane = lax.broadcasted_iota(jnp.int32, (1, 1, tile), 2)
    right = jnp.swapaxes(env_right[0], 1, 2)
    right = [jnp.where(lane < right_size[:, None, None], right, 0).astype(jnp.bfloat16)]
    for _ in range(RING - 1):
        right.append(hop(right[-1], "y"))
    right += [swap_cores(block) for block in right]
    loc = lax.all_to_all(
        jnp.broadcast_to(right_loc[:, 0][None, None], (STATES, 1, tiles)), "col", 0, 0, tiled=True
    )

    axis_blocks = (shard, behind_x, far_x, ahead_x, behind_z, far_z, ahead_z)
    corner_a = jnp.stack([block[:, :, :cut] for block in axis_blocks[1:4]])
    corner_b = jnp.stack([block[:, :, cut:] for block in axis_blocks[4:]])
    behind_a, behind_b = hop(corner_a, "z", 1), hop(corner_b, "x", 1)
    ahead_a, ahead_b = hop(corner_a, "z", -1), hop(corner_b, "x", -1)
    part_axis = left_parts(axis_kernel, len(AXIS), src, left, axis_blocks)
    behind_a, behind_b, part_axis = lax.optimization_barrier((behind_a, behind_b, part_axis))
    far_a, far_b = hop(behind_a, "z", 1), hop(behind_b, "x", 1)
    near = (behind_a, ahead_a, behind_b, ahead_b)
    part_near = left_parts(near_kernel, len(NEAR), src, left, near)

    pieces = (behind_a, ahead_a, far_a, behind_b, ahead_b, far_b)
    token, sums = jnp.zeros((16, 128), jnp.bfloat16), {}
    for chosen in CALLS:
        *outs, token = apply_terms(
            chosen, src, loc, two_site, token, left, right, pieces, (part_axis, part_near)
        )
        token = swap_cores(token)
        for number, a in enumerate(chosen):
            sums[a] = ring_sum(outs[RING * number : RING * (number + 1)], "z" if a < 2 else "x")
    summed = jnp.concatenate(
        [last_sum((sums[0], sums[1]), "x"), last_sum((sums[2], sums[3]), "z")]
    )
    row = lax.broadcasted_iota(jnp.int32, (1, tile, 1), 1)
    inside = row < left_size[:, None, None]
    return jnp.where(inside, summed, 0).astype(jnp.bfloat16)[:, None]


def solution(mesh):
    placed = (
        P("row", "col", None, None),
        P("col", "row", None, None, None),
        P("col", "row", None),
        P("col", None, None),
        P("col", "row", None, None),
        P("row", "col"),
        P("row"),
        P("row"),
    )
    return jax.shard_map(
        per_device,
        mesh=mesh,
        in_specs=placed,
        out_specs=P("row", "col", None, None),
        check_vma=False,
    )
```

```python
import functools

import jax
import jax.numpy as jnp
from jax import lax
from jax.experimental import pallas as pl
from jax.experimental.pallas import tpu as pltpu
from jax.sharding import PartitionSpec as P

BAND = 16
RING = 4
STATES = RING * RING
CORES = 2
LIMIT = 48 << 20
CALLS = ((0, 2), (1, 3))
WAYS = (1, -1)
AXIS = ((0, 0), (0, 1), (0, 2), (0, 3), (1, 0), (2, 0), (3, 0))
NEAR = ((1, 1), (1, 3), (3, 1), (3, 3))
FAR = ((1, 2), (2, 1), (2, 2), (2, 3), (3, 2))

HBM = pl.BlockSpec(memory_space=pltpu.HBM)
SMEM = pl.BlockSpec(memory_space=pltpu.SMEM)
VMEM = pl.BlockSpec(memory_space=pltpu.VMEM)


def in_hbm(value):
    return pltpu.with_memory_space_constraint(value, pltpu.HBM)


def hop(value, axis, distance=1):
    return ring_send(value, axis, (distance, -distance))


def shift(value, axis, distance):
    return ring_send(value, axis, (distance, distance))


def ring_send(value, axis, distances):
    pairs = []
    for row in range(RING * CORES):
        for col in range(STATES):
            step = distances[row % CORES]
            y, z, x = row // CORES, col // RING, col % RING
            y, z, x = (
                (v + (step if name == axis else 0)) % RING
                for name, v in (("y", y), ("z", z), ("x", x))
            )
            target = (y * CORES + row % CORES) * STATES + z * RING + x
            pairs.append((row * STATES + col, target))
    return lax.ppermute(value, ("row", "col"), pairs)


def swap_cores(value):
    return lax.ppermute(value, "row", [(r, r ^ 1) for r in range(RING * CORES)])


def add(*parts):
    total = parts[0].astype(jnp.float32)
    for part in parts[1:]:
        total += part.astype(jnp.float32)
    return total.astype(jnp.bfloat16)


def left_product(left, src_ref, a, block):
    rows = jnp.concatenate([block(src_ref[a, k]) for k in range(2)], axis=0)
    wide = jnp.concatenate([left[a, 0], left[a, 1]], axis=1)
    return jnp.dot(wide, rows, preferred_element_type=jnp.float32).astype(jnp.bfloat16)


def joined(first, second):
    return lambda j: jnp.concatenate([first[j], second[j]], axis=1)


def axis_kernel(src_ref, left_hbm, *refs):
    count = len(AXIS)
    blocks_hbm, out_hbm, (left, blocks, out, sem) = refs[:count], refs[count], refs[count + 1 :]
    get_left = pltpu.make_async_copy(left_hbm, left, sem.at[0])
    gets = [
        pltpu.make_async_copy(blocks_hbm[n], blocks.at[n], sem.at[1 + n]) for n in range(count)
    ]
    puts = [
        pltpu.make_async_copy(out.at[n], out_hbm.at[n], sem.at[1 + count + n])
        for n in range(count)
    ]
    get_left.start()
    for get in gets:
        get.start()
    get_left.wait()
    for n in range(count):
        gets[n].wait()
        for a in range(left.shape[0]):
            out[n, a] = left_product(left, src_ref, a, lambda j: blocks[n, j])
        puts[n].start()
    for put in puts:
        put.wait()


def near_kernel(src_ref, left_hbm, *refs):
    pieces_hbm, out_hbm, (left, pieces, out, sem) = refs[:4], refs[4], refs[5:]
    get_left = pltpu.make_async_copy(left_hbm, left, sem.at[0])
    gets = [pltpu.make_async_copy(pieces_hbm[n], pieces.at[n], sem.at[1 + n]) for n in range(4)]
    puts = [pltpu.make_async_copy(out.at[n], out_hbm.at[n], sem.at[5 + n]) for n in range(4)]
    for get in [get_left] + gets:
        get.start()
    for get in [get_left] + gets:
        get.wait()
    for n, (i, k) in enumerate(NEAR):
        block = joined(pieces.at[i // 2, k - 1], pieces.at[2 + k // 2, i - 1])
        for a in range(left.shape[0]):
            out[n, a] = left_product(left, src_ref, a, block)
        puts[n].start()
    for put in puts:
        put.wait()


def left_parts(kernel, count, src, left, pieces):
    tiles, _, tile, _ = left.shape
    out = (count, tiles, tile, tile)
    return pl.pallas_call(
        kernel,
        out_shape=pltpu.HBM(out, jnp.bfloat16),
        in_specs=[SMEM] + [HBM] * (1 + len(pieces)),
        out_specs=HBM,
        scratch_shapes=[
            pltpu.VMEM(left.shape, jnp.bfloat16),
            pltpu.VMEM((len(pieces),) + pieces[0].shape, jnp.bfloat16),
            pltpu.VMEM(out, jnp.bfloat16),
            pltpu.SemaphoreType.DMA((1 + len(pieces) + count,)),
        ],
        compiler_params=pltpu.CompilerParams(vmem_limit_bytes=LIMIT),
        cost_estimate=pl.CostEstimate(
            flops=count * tiles * 4 * tile**3, bytes_accessed=5 << 20, transcendentals=0
        ),
        name="left_parts",
    )(src, left, *(in_hbm(piece) for piece in pieces))


def mix_matrix(two_site, z, x, flow):
    size = STATES * BAND
    slot = lax.broadcasted_iota(jnp.int32, (size, STATES), 0) // BAND
    lane = lax.broadcasted_iota(jnp.int32, (size, STATES), 1)
    target = ((z + slot // RING) & 3) * RING + ((x + slot % RING) & 3)
    source = jnp.zeros_like(slot)
    for n, (i, k) in enumerate(AXIS + NEAR + FAR):
        state = ((z - flow * i) & 3) * RING + ((x - flow * k) & 3)
        source = jnp.where(slot == n, state, source)
    spread = lambda state: jnp.where(state == lane, 1.0, 0.0).astype(jnp.bfloat16)
    half = jnp.dot(spread(target), two_site, preferred_element_type=jnp.float32)
    full = lax.dot_general(
        half.astype(jnp.bfloat16),
        spread(source),
        (((1,), (1,)), ((), ())),
        preferred_element_type=jnp.float32,
    )
    row = lax.broadcasted_iota(jnp.int32, (size, size), 0)
    col = lax.broadcasted_iota(jnp.int32, (size, size), 1)
    return jnp.where(row % BAND == col % BAND, full, 0.0).astype(jnp.bfloat16)


def term(mixed, right, loc_ref, a, state, spot):
    z, x, y, core, flow = spot
    i, k = state
    t = ((z + i) & 3) * RING + ((x + k) & 3)
    group = t // 2
    other = (group + core) & 1
    back = (flow * (1 - 2 * other) * (y - group // CORES)) & 3
    tile = (other * RING + back) * 4 + loc_ref[t, 0, a]
    return jnp.dot(mixed, right[tile], preferred_element_type=jnp.float32).astype(jnp.bfloat16)


def spot_of():
    c, r = lax.axis_index("col"), lax.axis_index("row")
    core = r % CORES
    return c // RING, c % RING, r // CORES, core, 1 - 2 * core


def slot_state(half, ahead, inner):
    return (ahead, inner) if half == 0 else (inner, ahead)


def apply_kernel(chosen, src_ref, loc_ref, two_site_ref, token_ref, left_hbm, *refs):
    right_hbm, pieces_hbm, near_hbm, refs = refs[:8], refs[8:14], refs[14:16], refs[16:]
    outs, (left, right, first, second, part, mix, mixed, sem) = refs[:-8], refs[-8:]
    tile = left.shape[-1]
    spot = spot_of()
    z, x, _, _, flow = spot
    outs, passed = outs[:-1], outs[-1]
    passed[...] = token_ref[...]

    gets = [pltpu.make_async_copy(left_hbm, left, sem.at[0])]
    for which, pieces in enumerate((first, second)):
        behind, ahead, far = pieces_hbm[3 * which : 3 * which + 3]
        gets += [
            pltpu.make_async_copy(behind.at[1], pieces.at[0, 1], sem.at[1 + 3 * which]),
            pltpu.make_async_copy(ahead.at[1], pieces.at[2, 1], sem.at[2 + 3 * which]),
            pltpu.make_async_copy(far, pieces.at[1], sem.at[3 + 3 * which]),
        ]
    get_right = [
        pltpu.make_async_copy(right_hbm[n], right.at[pl.ds(4 * n, 4)], sem.at[7 + n])
        for n in range(8)
    ]
    get_near = [
        [
            pltpu.make_async_copy(
                near_hbm[0].at[:, a], part.at[place, pl.ds(0, 7)], sem.at[15 + 2 * place]
            ),
            pltpu.make_async_copy(
                near_hbm[1].at[:, a], part.at[place, pl.ds(7, 4)], sem.at[16 + 2 * place]
            ),
        ]
        for place, a in enumerate(chosen)
    ]
    for get in gets + get_near[0] + get_right:
        get.start()
    for later in get_near[1:]:
        for get in later:
            get.start()
    mix[...] = mix_matrix(two_site_ref[0], z, x, flow)
    for get in gets:
        get.wait()

    order = AXIS + NEAR + FAR
    for number, a in enumerate(chosen):
        half, way = a // 2, WAYS[a % 2]
        for n, (i, k) in enumerate(FAR):
            block = joined(first.at[i - 1, k - 1], second.at[k - 1, i - 1])
            part[number, len(AXIS) + len(NEAR) + n] = left_product(left, src_ref, a, block)
        for get in get_near[number]:
            get.wait()
        for band in range(tile // BAND):
            rows = pl.ds(band * BAND, BAND)
            stacked = part[number, :, rows, :].reshape(STATES * BAND, tile)
            product = jnp.dot(mix[...], stacked, preferred_element_type=jnp.float32)
            mixed[:, rows, :] = product.astype(jnp.bfloat16).reshape(STATES, BAND, tile)
        if number == 0:
            for get in get_right:
                get.wait()
        for ring in (2, 3, 1, 0):
            for inner in range(RING):
                i, k = slot_state(half, (way * ring) & 3, inner)
                outs[number * RING + ring][inner] = term(
                    mixed[i * RING + k], right, loc_ref, a, (i, k), spot
                )


def apply_terms(chosen, src, loc, two_site, token, left, right, pieces, near):
    tiles, _, tile, _ = left.shape
    count = len(chosen)
    out = jax.ShapeDtypeStruct((RING, tile, tile), jnp.bfloat16)
    side = (RING - 1, RING - 1) + pieces[0].shape[1:]
    return pl.pallas_call(
        functools.partial(apply_kernel, chosen),
        out_shape=[out] * (RING * count) + [jax.ShapeDtypeStruct(token.shape, token.dtype)],
        in_specs=[SMEM, SMEM, VMEM, VMEM] + [HBM] * 17,
        out_specs=[VMEM] * (RING * count + 1),
        scratch_shapes=[
            pltpu.VMEM(left.shape, jnp.bfloat16),
            pltpu.VMEM((32, tile, tile), jnp.bfloat16),
            pltpu.VMEM(side, jnp.bfloat16),
            pltpu.VMEM(side, jnp.bfloat16),
            pltpu.VMEM((count, STATES, tile, tile), jnp.bfloat16),
            pltpu.VMEM((STATES * BAND, STATES * BAND), jnp.bfloat16),
            pltpu.VMEM((STATES, tile, tile), jnp.bfloat16),
            pltpu.SemaphoreType.DMA((15 + 2 * count,)),
        ],
        compiler_params=pltpu.CompilerParams(vmem_limit_bytes=LIMIT),
        cost_estimate=pl.CostEstimate(
            flops=count * 80 * tile**3, bytes_accessed=8 << 20, transcendentals=0
        ),
        name="apply_terms",
    )(src, loc, two_site, token, left, *(in_hbm(v) for v in (*right, *pieces, *near)))


def ring_sum(blocks, axis, way):
    own, behind, far, ahead = blocks
    moving, straight = lax.optimization_barrier(
        (shift(far, axis, way), shift(ahead, axis, -way))
    )
    return own, straight, shift(add(behind, moving), axis, way)


def last_sum(tiles, axis):
    blocks = [
        jnp.stack([add(*(part[n] for part in parts)) for parts in tiles]) for n in range(RING)
    ]
    return add(blocks[0], *(shift(blocks[step], axis, step) for step in (2, 1, 3)))


def per_device(
    wavefunction, env_left, left_src, two_site, env_right, right_loc, left_size, right_size
):
    tile = wavefunction.shape[3]
    tiles = wavefunction.shape[0]
    src, left = left_src[0], env_left[0]

    shard, cut = wavefunction[:, 0], tile // 2
    behind_x, behind_z = hop(shard, "x", 1), hop(shard, "z", 1)
    ahead_x, ahead_z = hop(shard, "x", -1), hop(shard, "z", -1)
    far_x, far_z = hop(behind_x, "x", 1), hop(behind_z, "z", 1)

    loc = lax.all_to_all(
        jnp.broadcast_to(right_loc[:, 0][None, None], (STATES, 1, tiles)), "col", 0, 0, tiled=True
    )
    env_right, _ = lax.optimization_barrier((env_right, behind_x))
    lane = lax.broadcasted_iota(jnp.int32, (1, 1, tile), 2)
    right = jnp.swapaxes(env_right[0], 1, 2)
    right = jnp.where(lane < right_size[:, None, None], right, 0).astype(jnp.bfloat16)
    right_behind, right_ahead = hop(right, "y", 1), hop(right, "y", -1)
    right = [right, right_behind, hop(right_behind, "y", 1), right_ahead]
    right += [swap_cores(block) for block in right]
    far_x, far_z, loc = lax.optimization_barrier((far_x, far_z, loc))

    axis_blocks = (shard, behind_x, far_x, ahead_x, behind_z, far_z, ahead_z)
    corner_a = jnp.stack([block[:, :, :cut] for block in axis_blocks[1:4]])
    corner_b = jnp.stack([block[:, :, cut:] for block in axis_blocks[4:]])
    behind_a, behind_b = hop(corner_a, "z", 1), hop(corner_b, "x", 1)
    ahead_a, ahead_b = hop(corner_a, "z", -1), hop(corner_b, "x", -1)
    part_axis = left_parts(axis_kernel, len(AXIS), src, left, axis_blocks)
    far_a, far_b = hop(behind_a, "z", 1), hop(behind_b, "x", 1)
    near = (behind_a, ahead_a, behind_b, ahead_b)
    part_near = left_parts(near_kernel, len(NEAR), src, left, near)

    pieces = (behind_a, ahead_a, far_a, behind_b, ahead_b, far_b)
    token, sums = jnp.zeros((16, 128), jnp.bfloat16), {}
    for chosen in CALLS:
        *outs, token = apply_terms(
            chosen, src, loc, two_site, token, left, right, pieces, (part_axis, part_near)
        )
        token = swap_cores(token)
        for number, a in enumerate(chosen):
            blocks, axis = outs[RING * number : RING * (number + 1)], "z" if a < 2 else "x"
            sums[a] = ring_sum(blocks, axis, WAYS[a % 2])
    summed = jnp.concatenate(
        [last_sum((sums[0], sums[1]), "x"), last_sum((sums[2], sums[3]), "z")]
    )
    row = lax.broadcasted_iota(jnp.int32, (1, tile, 1), 1)
    inside = row < left_size[:, None, None]
    return jnp.where(inside, summed, 0).astype(jnp.bfloat16)[:, None]


def solution(mesh):
    placed = (
        P("row", "col", None, None),
        P("col", "row", None, None, None),
        P("col", "row", None),
        P("col", None, None),
        P("col", "row", None, None),
        P("row", "col"),
        P("row"),
        P("row"),
    )
    return jax.shard_map(
        per_device,
        mesh=mesh,
        in_specs=placed,
        out_specs=P("row", "col", None, None),
        check_vma=False,
    )
```

```python
import functools

import jax
import jax.numpy as jnp
from jax import lax
from jax.experimental import pallas as pl
from jax.experimental.pallas import tpu as pltpu
from jax.sharding import PartitionSpec as P

BAND = 16
RING = 4
STATES = RING * RING
CORES = 2
LIMIT = 48 << 20
CALLS = ((0, 2), (1, 3))
WAYS = (1, -1)
AXIS = ((0, 0), (0, 1), (0, 2), (0, 3), (1, 0), (2, 0), (3, 0))
NEAR = ((1, 1), (1, 3), (3, 1), (3, 3))
FAR = ((1, 2), (2, 1), (2, 2), (2, 3), (3, 2))

HBM = pl.BlockSpec(memory_space=pltpu.HBM)
SMEM = pl.BlockSpec(memory_space=pltpu.SMEM)
VMEM = pl.BlockSpec(memory_space=pltpu.VMEM)


def in_hbm(value):
    return pltpu.with_memory_space_constraint(value, pltpu.HBM)


def hop(value, axis, distance=1):
    return ring_send(value, axis, (distance, -distance))


def shift(value, axis, distance):
    return ring_send(value, axis, (distance, distance))


def ring_send(value, axis, distances):
    pairs = []
    for row in range(RING * CORES):
        for col in range(STATES):
            step = distances[row % CORES]
            y, z, x = row // CORES, col // RING, col % RING
            y, z, x = (
                (v + (step if name == axis else 0)) % RING
                for name, v in (("y", y), ("z", z), ("x", x))
            )
            target = (y * CORES + row % CORES) * STATES + z * RING + x
            pairs.append((row * STATES + col, target))
    return lax.ppermute(value, ("row", "col"), pairs)


def swap_cores(value):
    return lax.ppermute(value, "row", [(r, r ^ 1) for r in range(RING * CORES)])


def add(*parts):
    total = parts[0].astype(jnp.float32)
    for part in parts[1:]:
        total += part.astype(jnp.float32)
    return total.astype(jnp.bfloat16)


def left_product(left, src_ref, a, block):
    rows = jnp.concatenate([block(src_ref[a, k]) for k in range(2)], axis=0)
    wide = jnp.concatenate([left[a, 0], left[a, 1]], axis=1)
    return jnp.dot(wide, rows, preferred_element_type=jnp.float32).astype(jnp.bfloat16)


def joined(first, second):
    return lambda j: jnp.concatenate([first[j], second[j]], axis=1)


def axis_kernel(src_ref, left_hbm, *refs):
    count = len(AXIS)
    blocks_hbm, out_hbm, (left, blocks, out, sem) = refs[:count], refs[count], refs[count + 1 :]
    get_left = pltpu.make_async_copy(left_hbm, left, sem.at[0])
    gets = [
        pltpu.make_async_copy(blocks_hbm[n], blocks.at[n], sem.at[1 + n]) for n in range(count)
    ]
    puts = [
        pltpu.make_async_copy(out.at[n], out_hbm.at[n], sem.at[1 + count + n])
        for n in range(count)
    ]
    get_left.start()
    for get in gets:
        get.start()
    get_left.wait()
    for n in range(count):
        gets[n].wait()
        for a in range(left.shape[0]):
            out[n, a] = left_product(left, src_ref, a, lambda j: blocks[n, j])
        puts[n].start()
    for put in puts:
        put.wait()


def near_kernel(src_ref, left_hbm, *refs):
    pieces_hbm, out_hbm, (left, pieces, out, sem) = refs[:4], refs[4], refs[5:]
    get_left = pltpu.make_async_copy(left_hbm, left, sem.at[0])
    gets = [pltpu.make_async_copy(pieces_hbm[n], pieces.at[n], sem.at[1 + n]) for n in range(4)]
    puts = [pltpu.make_async_copy(out.at[n], out_hbm.at[n], sem.at[5 + n]) for n in range(4)]
    for get in [get_left] + gets:
        get.start()
    for get in [get_left] + gets:
        get.wait()
    for n, (i, k) in enumerate(NEAR):
        block = joined(pieces.at[i // 2, k - 1], pieces.at[2 + k // 2, i - 1])
        for a in range(left.shape[0]):
            out[n, a] = left_product(left, src_ref, a, block)
        puts[n].start()
    for put in puts:
        put.wait()


def join_kernel(start, first, second, third, out, sem):
    cols = pl.ds(start, out.shape[-1])
    copies = [
        pltpu.make_async_copy(block.at[:, :, cols], out.at[n], sem.at[n])
        for n, block in enumerate((first, second, third))
    ]
    for copy in copies:
        copy.start()
    for copy in copies:
        copy.wait()


def join(blocks, start):
    tiles, tile, _ = blocks[0].shape
    return pl.pallas_call(
        functools.partial(join_kernel, start),
        out_shape=jax.ShapeDtypeStruct((len(blocks), tiles, tile, tile // 2), jnp.bfloat16),
        in_specs=[pl.BlockSpec(memory_space=pl.ANY)] * 3,
        out_specs=VMEM,
        scratch_shapes=[pltpu.SemaphoreType.DMA((3,))],
        compiler_params=pltpu.CompilerParams(vmem_limit_bytes=4 << 20),
        cost_estimate=pl.CostEstimate(flops=1, bytes_accessed=1 << 19, transcendentals=0),
        name="join",
    )(*blocks)


def left_parts(kernel, count, src, left, pieces):
    tiles, _, tile, _ = left.shape
    out = (count, tiles, tile, tile)
    return pl.pallas_call(
        kernel,
        out_shape=pltpu.HBM(out, jnp.bfloat16),
        in_specs=[SMEM] + [HBM] * (1 + len(pieces)),
        out_specs=HBM,
        scratch_shapes=[
            pltpu.VMEM(left.shape, jnp.bfloat16),
            pltpu.VMEM((len(pieces),) + pieces[0].shape, jnp.bfloat16),
            pltpu.VMEM(out, jnp.bfloat16),
            pltpu.SemaphoreType.DMA((1 + len(pieces) + count,)),
        ],
        compiler_params=pltpu.CompilerParams(vmem_limit_bytes=LIMIT),
        cost_estimate=pl.CostEstimate(
            flops=count * tiles * 4 * tile**3, bytes_accessed=5 << 20, transcendentals=0
        ),
        name="left_parts",
    )(src, left, *(in_hbm(piece) for piece in pieces))


def mix_matrix(two_site, z, x, flow):
    size = STATES * BAND
    slot = lax.broadcasted_iota(jnp.int32, (size, STATES), 0) // BAND
    lane = lax.broadcasted_iota(jnp.int32, (size, STATES), 1)
    target = ((z + slot // RING) & 3) * RING + ((x + slot % RING) & 3)
    source = jnp.zeros_like(slot)
    for n, (i, k) in enumerate(AXIS + NEAR + FAR):
        state = ((z - flow * i) & 3) * RING + ((x - flow * k) & 3)
        source = jnp.where(slot == n, state, source)
    spread = lambda state: jnp.where(state == lane, 1.0, 0.0).astype(jnp.bfloat16)
    half = jnp.dot(spread(target), two_site, preferred_element_type=jnp.float32)
    full = lax.dot_general(
        half.astype(jnp.bfloat16),
        spread(source),
        (((1,), (1,)), ((), ())),
        preferred_element_type=jnp.float32,
    )
    row = lax.broadcasted_iota(jnp.int32, (size, size), 0)
    col = lax.broadcasted_iota(jnp.int32, (size, size), 1)
    return jnp.where(row % BAND == col % BAND, full, 0.0).astype(jnp.bfloat16)


def term(mixed, right, loc_ref, a, state, spot):
    z, x, y, core, flow = spot
    i, k = state
    t = ((z + i) & 3) * RING + ((x + k) & 3)
    group = t // 2
    other = (group + core) & 1
    back = (flow * (1 - 2 * other) * (y - group // CORES)) & 3
    tile = (other * RING + back) * 4 + loc_ref[t, 0, a]
    return jnp.dot(mixed, right[tile], preferred_element_type=jnp.float32).astype(jnp.bfloat16)


def spot_of():
    c, r = lax.axis_index("col"), lax.axis_index("row")
    core = r % CORES
    return c // RING, c % RING, r // CORES, core, 1 - 2 * core


def slot_state(half, ahead, inner):
    return (ahead, inner) if half == 0 else (inner, ahead)


def apply_kernel(chosen, src_ref, loc_ref, two_site_ref, token_ref, left_hbm, *refs):
    right_hbm, pieces_hbm, near_hbm, refs = refs[:8], refs[8:14], refs[14:16], refs[16:]
    outs, (left, right, first, second, part, mix, mixed, sem) = refs[:-8], refs[-8:]
    tile = left.shape[-1]
    spot = spot_of()
    z, x, _, _, flow = spot
    outs, passed = outs[:-1], outs[-1]
    passed[...] = token_ref[...]

    gets = [pltpu.make_async_copy(left_hbm, left, sem.at[0])]
    for which, pieces in enumerate((first, second)):
        behind, ahead, far = pieces_hbm[3 * which : 3 * which + 3]
        gets += [
            pltpu.make_async_copy(behind.at[1], pieces.at[0, 1], sem.at[1 + 3 * which]),
            pltpu.make_async_copy(ahead.at[1], pieces.at[2, 1], sem.at[2 + 3 * which]),
            pltpu.make_async_copy(far, pieces.at[1], sem.at[3 + 3 * which]),
        ]
    get_right = [
        pltpu.make_async_copy(right_hbm[n], right.at[pl.ds(4 * n, 4)], sem.at[7 + n])
        for n in range(8)
    ]
    get_near = [
        [
            pltpu.make_async_copy(
                near_hbm[0].at[:, a], part.at[place, pl.ds(0, 7)], sem.at[15 + 2 * place]
            ),
            pltpu.make_async_copy(
                near_hbm[1].at[:, a], part.at[place, pl.ds(7, 4)], sem.at[16 + 2 * place]
            ),
        ]
        for place, a in enumerate(chosen)
    ]
    for get in gets + get_near[0] + get_right:
        get.start()
    for later in get_near[1:]:
        for get in later:
            get.start()
    mix[...] = mix_matrix(two_site_ref[0], z, x, flow)
    for get in gets:
        get.wait()

    order = AXIS + NEAR + FAR
    for number, a in enumerate(chosen):
        half, way = a // 2, WAYS[a % 2]
        for n, (i, k) in enumerate(FAR):
            block = joined(first.at[i - 1, k - 1], second.at[k - 1, i - 1])
            part[number, len(AXIS) + len(NEAR) + n] = left_product(left, src_ref, a, block)
        for get in get_near[number]:
            get.wait()
        for band in range(tile // BAND):
            rows = pl.ds(band * BAND, BAND)
            stacked = part[number, :, rows, :].reshape(STATES * BAND, tile)
            product = jnp.dot(mix[...], stacked, preferred_element_type=jnp.float32)
            mixed[:, rows, :] = product.astype(jnp.bfloat16).reshape(STATES, BAND, tile)
        if number == 0:
            for get in get_right:
                get.wait()
        for ring in (2, 3, 1, 0):
            for inner in range(RING):
                i, k = slot_state(half, (way * ring) & 3, inner)
                outs[number * RING + ring][inner] = term(
                    mixed[i * RING + k], right, loc_ref, a, (i, k), spot
                )


def apply_terms(chosen, src, loc, two_site, token, left, right, pieces, near):
    tiles, _, tile, _ = left.shape
    count = len(chosen)
    out = jax.ShapeDtypeStruct((RING, tile, tile), jnp.bfloat16)
    side = (RING - 1, RING - 1) + pieces[0].shape[1:]
    return pl.pallas_call(
        functools.partial(apply_kernel, chosen),
        out_shape=[out] * (RING * count) + [jax.ShapeDtypeStruct(token.shape, token.dtype)],
        in_specs=[SMEM, SMEM, VMEM, VMEM] + [HBM] * 17,
        out_specs=[VMEM] * (RING * count + 1),
        scratch_shapes=[
            pltpu.VMEM(left.shape, jnp.bfloat16),
            pltpu.VMEM((32, tile, tile), jnp.bfloat16),
            pltpu.VMEM(side, jnp.bfloat16),
            pltpu.VMEM(side, jnp.bfloat16),
            pltpu.VMEM((count, STATES, tile, tile), jnp.bfloat16),
            pltpu.VMEM((STATES * BAND, STATES * BAND), jnp.bfloat16),
            pltpu.VMEM((STATES, tile, tile), jnp.bfloat16),
            pltpu.SemaphoreType.DMA((15 + 2 * count,)),
        ],
        compiler_params=pltpu.CompilerParams(vmem_limit_bytes=LIMIT),
        cost_estimate=pl.CostEstimate(
            flops=count * 80 * tile**3, bytes_accessed=8 << 20, transcendentals=0
        ),
        name="apply_terms",
    )(src, loc, two_site, token, left, *(in_hbm(v) for v in (*right, *pieces, *near)))


def ring_sum(blocks, axis, way):
    own, behind, far, ahead = blocks
    moving, straight = lax.optimization_barrier(
        (shift(far, axis, way), shift(ahead, axis, -way))
    )
    return own, straight, shift(add(behind, moving), axis, way)


def last_sum(tiles, axis):
    blocks = [
        jnp.stack([add(*(part[n] for part in parts)) for parts in tiles]) for n in range(RING)
    ]
    return add(blocks[0], *(shift(blocks[step], axis, step) for step in (2, 1, 3)))


def per_device(
    wavefunction, env_left, left_src, two_site, env_right, right_loc, left_size, right_size
):
    tile = wavefunction.shape[3]
    tiles = wavefunction.shape[0]
    src, left = left_src[0], env_left[0]

    shard, cut = wavefunction[:, 0], tile // 2
    behind_x, behind_z = hop(shard, "x", 1), hop(shard, "z", 1)
    ahead_x, ahead_z = hop(shard, "x", -1), hop(shard, "z", -1)
    behind_x, ahead_x = lax.optimization_barrier((behind_x, ahead_x))
    behind_z, ahead_z = lax.optimization_barrier((behind_z, ahead_z))
    far_x, far_z = hop(behind_x, "x", 1), hop(behind_z, "z", 1)

    loc = lax.all_to_all(
        jnp.broadcast_to(right_loc[:, 0][None, None], (STATES, 1, tiles)), "col", 0, 0, tiled=True
    )
    env_right, loc, _ = lax.optimization_barrier((env_right, loc, behind_x))
    lane = lax.broadcasted_iota(jnp.int32, (1, 1, tile), 2)
    right = jnp.swapaxes(env_right[0], 1, 2)
    right = jnp.where(lane < right_size[:, None, None], right, 0).astype(jnp.bfloat16)
    right = [right]
    for _ in range(RING - 1):
        right.append(hop(right[-1], "y"))
    right += [swap_cores(block) for block in right]

    axis_blocks = (shard, behind_x, far_x, ahead_x, behind_z, far_z, ahead_z)
    corner_a, corner_b = join(axis_blocks[1:4], 0), join(axis_blocks[4:], cut)
    behind_a, behind_b = hop(corner_a, "z", 1), hop(corner_b, "x", 1)
    ahead_a, ahead_b = hop(corner_a, "z", -1), hop(corner_b, "x", -1)
    part_axis = left_parts(axis_kernel, len(AXIS), src, left, axis_blocks)
    far_a, far_b = hop(behind_a, "z", 1), hop(behind_b, "x", 1)
    near = (behind_a, ahead_a, behind_b, ahead_b)
    part_near = left_parts(near_kernel, len(NEAR), src, left, near)

    pieces = (behind_a, ahead_a, far_a, behind_b, ahead_b, far_b)
    token, sums = jnp.zeros((16, 128), jnp.bfloat16), {}
    for chosen in CALLS:
        *outs, token = apply_terms(
            chosen, src, loc, two_site, token, left, right, pieces, (part_axis, part_near)
        )
        token = swap_cores(token)
        for number, a in enumerate(chosen):
            blocks, axis = outs[RING * number : RING * (number + 1)], "z" if a < 2 else "x"
            sums[a] = ring_sum(blocks, axis, WAYS[a % 2])
    summed = jnp.concatenate(
        [last_sum((sums[0], sums[1]), "x"), last_sum((sums[2], sums[3]), "z")]
    )
    row = lax.broadcasted_iota(jnp.int32, (1, tile, 1), 1)
    inside = row < left_size[:, None, None]
    return jnp.where(inside, summed, 0).astype(jnp.bfloat16)[:, None]


def solution(mesh):
    placed = (
        P("row", "col", None, None),
        P("col", "row", None, None, None),
        P("col", "row", None),
        P("col", None, None),
        P("col", "row", None, None),
        P("row", "col"),
        P("row"),
        P("row"),
    )
    return jax.shard_map(
        per_device,
        mesh=mesh,
        in_specs=placed,
        out_specs=P("row", "col", None, None),
        check_vma=False,
    )
```

```python
import functools

import jax
import jax.numpy as jnp
from jax import lax
from jax.experimental import pallas as pl
from jax.experimental.pallas import tpu as pltpu
from jax.sharding import PartitionSpec as P

BAND = 16
RING = 4
STATES = RING * RING
CORES = 2
LIMIT = 48 << 20
CALLS = ((0, 2), (1, 3))
WAYS = (1, -1)
AXIS = ((0, 0), (0, 1), (0, 2), (0, 3), (1, 0), (2, 0), (3, 0))
NEAR = ((1, 1), (1, 3), (3, 1), (3, 3))
FAR = ((1, 2), (2, 1), (2, 2), (2, 3), (3, 2))

HBM = pl.BlockSpec(memory_space=pltpu.HBM)
SMEM = pl.BlockSpec(memory_space=pltpu.SMEM)
VMEM = pl.BlockSpec(memory_space=pltpu.VMEM)


def in_hbm(value):
    return pltpu.with_memory_space_constraint(value, pltpu.HBM)


def hop(value, axis, distance=1):
    return ring_send(value, axis, (distance, -distance))


def shift(value, axis, distance):
    return ring_send(value, axis, (distance, distance))


def ring_send(value, axis, distances):
    pairs = []
    for row in range(RING * CORES):
        for col in range(STATES):
            step = distances[row % CORES]
            y, z, x = row // CORES, col // RING, col % RING
            y, z, x = (
                (v + (step if name == axis else 0)) % RING
                for name, v in (("y", y), ("z", z), ("x", x))
            )
            target = (y * CORES + row % CORES) * STATES + z * RING + x
            pairs.append((row * STATES + col, target))
    return lax.ppermute(value, ("row", "col"), pairs)


def swap_cores(value):
    return lax.ppermute(value, "row", [(r, r ^ 1) for r in range(RING * CORES)])


def add(*parts):
    total = parts[0].astype(jnp.float32)
    for part in parts[1:]:
        total += part.astype(jnp.float32)
    return total.astype(jnp.bfloat16)


def left_product(left, src_ref, a, block):
    rows = jnp.concatenate([block(src_ref[a, k]) for k in range(2)], axis=0)
    wide = jnp.concatenate([left[a, 0], left[a, 1]], axis=1)
    return jnp.dot(wide, rows, preferred_element_type=jnp.float32).astype(jnp.bfloat16)


def joined(first, second):
    return lambda j: jnp.concatenate([first[j], second[j]], axis=1)


def axis_kernel(src_ref, left_hbm, *refs):
    count = len(AXIS)
    blocks_hbm, out_hbm, (left, blocks, out, sem) = refs[:count], refs[count], refs[count + 1 :]
    get_left = pltpu.make_async_copy(left_hbm, left, sem.at[0])
    gets = [
        pltpu.make_async_copy(blocks_hbm[n], blocks.at[n], sem.at[1 + n]) for n in range(count)
    ]
    puts = [
        pltpu.make_async_copy(out.at[n], out_hbm.at[n], sem.at[1 + count + n])
        for n in range(count)
    ]
    get_left.start()
    for get in gets:
        get.start()
    get_left.wait()
    for n in range(count):
        gets[n].wait()
        for a in range(left.shape[0]):
            out[n, a] = left_product(left, src_ref, a, lambda j: blocks[n, j])
        puts[n].start()
    for put in puts:
        put.wait()


def near_kernel(src_ref, left_hbm, *refs):
    pieces_hbm, out_hbm, (left, pieces, out, sem) = refs[:4], refs[4], refs[5:]
    get_left = pltpu.make_async_copy(left_hbm, left, sem.at[0])
    gets = [pltpu.make_async_copy(pieces_hbm[n], pieces.at[n], sem.at[1 + n]) for n in range(4)]
    puts = [pltpu.make_async_copy(out.at[n], out_hbm.at[n], sem.at[5 + n]) for n in range(4)]
    for get in [get_left] + gets:
        get.start()
    for get in [get_left] + gets:
        get.wait()
    for n, (i, k) in enumerate(NEAR):
        block = joined(pieces.at[i // 2, k - 1], pieces.at[2 + k // 2, i - 1])
        for a in range(left.shape[0]):
            out[n, a] = left_product(left, src_ref, a, block)
        puts[n].start()
    for put in puts:
        put.wait()


def join_kernel(start, first, second, third, out, sem):
    cols = pl.ds(start, out.shape[-1])
    copies = [
        pltpu.make_async_copy(block.at[:, :, cols], out.at[n], sem.at[n])
        for n, block in enumerate((first, second, third))
    ]
    for copy in copies:
        copy.start()
    for copy in copies:
        copy.wait()


def join(blocks, start):
    tiles, tile, _ = blocks[0].shape
    return pl.pallas_call(
        functools.partial(join_kernel, start),
        out_shape=jax.ShapeDtypeStruct((len(blocks), tiles, tile, tile // 2), jnp.bfloat16),
        in_specs=[pl.BlockSpec(memory_space=pl.ANY)] * 3,
        out_specs=VMEM,
        scratch_shapes=[pltpu.SemaphoreType.DMA((3,))],
        compiler_params=pltpu.CompilerParams(vmem_limit_bytes=4 << 20),
        cost_estimate=pl.CostEstimate(flops=1, bytes_accessed=1 << 19, transcendentals=0),
        name="join",
    )(*blocks)


def left_parts(kernel, count, src, left, pieces):
    tiles, _, tile, _ = left.shape
    out = (count, tiles, tile, tile)
    return pl.pallas_call(
        kernel,
        out_shape=pltpu.HBM(out, jnp.bfloat16),
        in_specs=[SMEM] + [HBM] * (1 + len(pieces)),
        out_specs=HBM,
        scratch_shapes=[
            pltpu.VMEM(left.shape, jnp.bfloat16),
            pltpu.VMEM((len(pieces),) + pieces[0].shape, jnp.bfloat16),
            pltpu.VMEM(out, jnp.bfloat16),
            pltpu.SemaphoreType.DMA((1 + len(pieces) + count,)),
        ],
        compiler_params=pltpu.CompilerParams(vmem_limit_bytes=LIMIT),
        cost_estimate=pl.CostEstimate(
            flops=count * tiles * 4 * tile**3, bytes_accessed=5 << 20, transcendentals=0
        ),
        name="left_parts",
    )(src, left, *(in_hbm(piece) for piece in pieces))


def mix_matrix(two_site, z, x, flow):
    size = STATES * BAND
    slot = lax.broadcasted_iota(jnp.int32, (size, STATES), 0) // BAND
    lane = lax.broadcasted_iota(jnp.int32, (size, STATES), 1)
    target = ((z + slot // RING) & 3) * RING + ((x + slot % RING) & 3)
    source = jnp.zeros_like(slot)
    for n, (i, k) in enumerate(AXIS + NEAR + FAR):
        state = ((z - flow * i) & 3) * RING + ((x - flow * k) & 3)
        source = jnp.where(slot == n, state, source)
    spread = lambda state: jnp.where(state == lane, 1.0, 0.0).astype(jnp.bfloat16)
    half = jnp.dot(spread(target), two_site, preferred_element_type=jnp.float32)
    full = lax.dot_general(
        half.astype(jnp.bfloat16),
        spread(source),
        (((1,), (1,)), ((), ())),
        preferred_element_type=jnp.float32,
    )
    row = lax.broadcasted_iota(jnp.int32, (size, size), 0)
    col = lax.broadcasted_iota(jnp.int32, (size, size), 1)
    return jnp.where(row % BAND == col % BAND, full, 0.0).astype(jnp.bfloat16)


def term(mixed, right, loc_ref, a, state, spot):
    z, x, y, core, flow = spot
    i, k = state
    t = ((z + i) & 3) * RING + ((x + k) & 3)
    group = t // 2
    other = (group + core) & 1
    back = (flow * (1 - 2 * other) * (y - group // CORES)) & 3
    tile = (other * RING + back) * 4 + loc_ref[t, 0, a]
    return lax.dot_general(
        mixed, right[tile], (((1,), (1,)), ((), ())), preferred_element_type=jnp.float32
    ).astype(jnp.bfloat16)


def spot_of():
    c, r = lax.axis_index("col"), lax.axis_index("row")
    core = r % CORES
    return c // RING, c % RING, r // CORES, core, 1 - 2 * core


def slot_state(half, ahead, inner):
    return (ahead, inner) if half == 0 else (inner, ahead)


def apply_kernel(chosen, src_ref, loc_ref, two_site_ref, token_ref, left_hbm, *refs):
    right_hbm, pieces_hbm, near_hbm, refs = refs[:8], refs[8:14], refs[14:16], refs[16:]
    outs, (left, right, first, second, part, mix, mixed, sem) = refs[:-8], refs[-8:]
    tile = left.shape[-1]
    spot = spot_of()
    z, x, _, _, flow = spot
    outs, passed = outs[:-1], outs[-1]
    passed[...] = token_ref[...]

    gets = [pltpu.make_async_copy(left_hbm, left, sem.at[0])]
    for which, pieces in enumerate((first, second)):
        behind, ahead, far = pieces_hbm[3 * which : 3 * which + 3]
        gets += [
            pltpu.make_async_copy(behind.at[1], pieces.at[0, 1], sem.at[1 + 3 * which]),
            pltpu.make_async_copy(ahead.at[1], pieces.at[2, 1], sem.at[2 + 3 * which]),
            pltpu.make_async_copy(far, pieces.at[1], sem.at[3 + 3 * which]),
        ]
    get_right = [
        pltpu.make_async_copy(right_hbm[n], right.at[pl.ds(4 * n, 4)], sem.at[7 + n])
        for n in range(8)
    ]
    get_near = [
        [
            pltpu.make_async_copy(
                near_hbm[0].at[:, a], part.at[place, pl.ds(0, 7)], sem.at[15 + 2 * place]
            ),
            pltpu.make_async_copy(
                near_hbm[1].at[:, a], part.at[place, pl.ds(7, 4)], sem.at[16 + 2 * place]
            ),
        ]
        for place, a in enumerate(chosen)
    ]
    for get in gets + get_near[0] + get_right:
        get.start()
    for later in get_near[1:]:
        for get in later:
            get.start()
    mix[...] = mix_matrix(two_site_ref[0], z, x, flow)
    for get in gets:
        get.wait()

    order = AXIS + NEAR + FAR
    for number, a in enumerate(chosen):
        half, way = a // 2, WAYS[a % 2]
        for n, (i, k) in enumerate(FAR):
            block = joined(first.at[i - 1, k - 1], second.at[k - 1, i - 1])
            part[number, len(AXIS) + len(NEAR) + n] = left_product(left, src_ref, a, block)
        for get in get_near[number]:
            get.wait()
        for band in range(tile // BAND):
            rows = pl.ds(band * BAND, BAND)
            stacked = part[number, :, rows, :].reshape(STATES * BAND, tile)
            product = jnp.dot(mix[...], stacked, preferred_element_type=jnp.float32)
            mixed[:, rows, :] = product.astype(jnp.bfloat16).reshape(STATES, BAND, tile)
        if number == 0:
            for get in get_right:
                get.wait()
        for ring in (2, 3, 1, 0):
            for inner in range(RING):
                i, k = slot_state(half, (way * ring) & 3, inner)
                outs[number * RING + ring][inner] = term(
                    mixed[i * RING + k], right, loc_ref, a, (i, k), spot
                )


def apply_terms(chosen, src, loc, two_site, token, left, right, pieces, near):
    tiles, _, tile, _ = left.shape
    count = len(chosen)
    out = jax.ShapeDtypeStruct((RING, tile, tile), jnp.bfloat16)
    side = (RING - 1, RING - 1) + pieces[0].shape[1:]
    return pl.pallas_call(
        functools.partial(apply_kernel, chosen),
        out_shape=[out] * (RING * count) + [jax.ShapeDtypeStruct(token.shape, token.dtype)],
        in_specs=[SMEM, SMEM, VMEM, VMEM] + [HBM] * 17,
        out_specs=[VMEM] * (RING * count + 1),
        scratch_shapes=[
            pltpu.VMEM(left.shape, jnp.bfloat16),
            pltpu.VMEM((32, tile, tile), jnp.bfloat16),
            pltpu.VMEM(side, jnp.bfloat16),
            pltpu.VMEM(side, jnp.bfloat16),
            pltpu.VMEM((count, STATES, tile, tile), jnp.bfloat16),
            pltpu.VMEM((STATES * BAND, STATES * BAND), jnp.bfloat16),
            pltpu.VMEM((STATES, tile, tile), jnp.bfloat16),
            pltpu.SemaphoreType.DMA((15 + 2 * count,)),
        ],
        compiler_params=pltpu.CompilerParams(vmem_limit_bytes=LIMIT),
        cost_estimate=pl.CostEstimate(
            flops=count * 80 * tile**3, bytes_accessed=8 << 20, transcendentals=0
        ),
        name="apply_terms",
    )(src, loc, two_site, token, left, *(in_hbm(v) for v in (*right, *pieces, *near)))


def ring_sum(blocks, axis, way):
    own, behind, far, ahead = blocks
    moving, straight = lax.optimization_barrier(
        (shift(far, axis, way), shift(ahead, axis, -way))
    )
    return own, straight, shift(add(behind, moving), axis, way)


def last_sum(tiles, axis):
    blocks = [
        jnp.stack([add(*(part[n] for part in parts)) for parts in tiles]) for n in range(RING)
    ]
    return add(blocks[0], *(shift(blocks[step], axis, step) for step in (2, 1, 3)))


def per_device(
    wavefunction, env_left, left_src, two_site, env_right, right_loc, left_size, right_size
):
    tile = wavefunction.shape[3]
    tiles = wavefunction.shape[0]
    src, left = left_src[0], env_left[0]

    shard, cut = wavefunction[:, 0], tile // 2
    behind_x, behind_z = hop(shard, "x", 1), hop(shard, "z", 1)
    ahead_x, ahead_z = hop(shard, "x", -1), hop(shard, "z", -1)
    behind_x, ahead_x = lax.optimization_barrier((behind_x, ahead_x))
    behind_z, ahead_z = lax.optimization_barrier((behind_z, ahead_z))
    far_x, far_z = hop(behind_x, "x", 1), hop(behind_z, "z", 1)

    loc = lax.all_to_all(
        jnp.broadcast_to(right_loc[:, 0][None, None], (STATES, 1, tiles)), "col", 0, 0, tiled=True
    )
    env_right, loc, _ = lax.optimization_barrier((env_right, loc, behind_x))
    line = lax.broadcasted_iota(jnp.int32, (1, tile, 1), 1)
    right = jnp.where(line < right_size[:, None, None], env_right[0], 0).astype(jnp.bfloat16)
    right = [right]
    for _ in range(RING - 1):
        right.append(hop(right[-1], "y"))
    right += [swap_cores(block) for block in right]

    axis_blocks = (shard, behind_x, far_x, ahead_x, behind_z, far_z, ahead_z)
    corner_a, corner_b = join(axis_blocks[1:4], 0), join(axis_blocks[4:], cut)
    behind_a, behind_b = hop(corner_a, "z", 1), hop(corner_b, "x", 1)
    ahead_a, ahead_b = hop(corner_a, "z", -1), hop(corner_b, "x", -1)
    part_axis = left_parts(axis_kernel, len(AXIS), src, left, axis_blocks)
    far_a, far_b = hop(behind_a, "z", 1), hop(behind_b, "x", 1)
    near = (behind_a, ahead_a, behind_b, ahead_b)
    part_near = left_parts(near_kernel, len(NEAR), src, left, near)

    pieces = (behind_a, ahead_a, far_a, behind_b, ahead_b, far_b)
    token, sums = jnp.zeros((16, 128), jnp.bfloat16), {}
    for chosen in CALLS:
        *outs, token = apply_terms(
            chosen, src, loc, two_site, token, left, right, pieces, (part_axis, part_near)
        )
        token = swap_cores(token)
        for number, a in enumerate(chosen):
            blocks, axis = outs[RING * number : RING * (number + 1)], "z" if a < 2 else "x"
            sums[a] = ring_sum(blocks, axis, WAYS[a % 2])
    summed = jnp.concatenate(
        [last_sum((sums[0], sums[1]), "x"), last_sum((sums[2], sums[3]), "z")]
    )
    row = lax.broadcasted_iota(jnp.int32, (1, tile, 1), 1)
    inside = row < left_size[:, None, None]
    return jnp.where(inside, summed, 0).astype(jnp.bfloat16)[:, None]


def solution(mesh):
    placed = (
        P("row", "col", None, None),
        P("col", "row", None, None, None),
        P("col", "row", None),
        P("col", None, None),
        P("col", "row", None, None),
        P("row", "col"),
        P("row"),
        P("row"),
    )
    return jax.shard_map(
        per_device,
        mesh=mesh,
        in_specs=placed,
        out_specs=P("row", "col", None, None),
        check_vma=False,
    )
```
